1024 devices in a mesh: dp: 8 (over x), wide: 16 (over y, core), narrow: 8 (over z).
Axes of the slice: x: 8, y: 8, z: 8, core: 2. Of those that a mesh axis runs over, the one named last changes fastest.
Arguments:
- out_grad: bfloat16 [16384, 2048], P(('dp', 'wide', 'narrow')), may hold values from -6 to 6
- routes: int32 [16384, 8], P(('dp', 'wide', 'narrow')), may hold values from 0 to 127, as said below
- gates: bfloat16 [16384, 8], P(('dp', 'wide', 'narrow')), may hold values from 0.029907227 to 0.59765625
- pre_gate: bfloat16 [8, 128, 256, 768], P('dp', ('wide', 'narrow')), may hold values from -5 to 5
- pre_up: bfloat16 [8, 128, 256, 768], P('dp', ('wide', 'narrow')), may hold values from -5 to 5
- down_weight: bfloat16 [128, 768, 2048], P(('wide', 'narrow')), may hold values from -0.125 to 0.125
Outputs:
- grad_down: bfloat16 [128, 768, 2048], P(('wide', 'narrow'), None, 'dp')
- grad_pre_gate: bfloat16 [8, 128, 256, 768], P('dp', ('wide', 'narrow'))
- grad_pre_up: bfloat16 [8, 128, 256, 768], P('dp', ('wide', 'narrow'))
- grad_gates: float32 [16384, 8], P(('dp', 'wide', 'narrow'))
The draws below stay inside these ranges and needn't reach their ends.
Inputs may be any that keep to these rules, and one draw needn't show every extreme that they name: `routes`: each token names 8 different experts. The tokens of one device name each expert either 0 or 2 times. In every group some expert is named 2 times by every device of the group.
All inputs are finite; a program needn't handle non-finite values.
Results may differ from the reference program's by a relative error of at most 0.012.
Values may be sent and summed in bfloat16 or wider, within the bound.
A program may use at most 32 MiB of HBM per device.

```python
import math
import jax
import jax.numpy as jnp
from jax import lax

D = 2048
FF = 768
TOPK = 8
TOK_DEV = 16
EXPERTS = 128
GROUPS = 8
TOKENS = 16384
CAP = 2
SLOTS = 256


def draw_routes(key, part):
    devices = TOKENS // TOK_DEV
    residues = EXPERTS // TOPK
    used_count = max(residues // 2, 1)
    key_perm = jax.random.fold_in(key, 11)
    key_order = jax.random.fold_in(key, 12)
    key_hot = jax.random.fold_in(key, 13)
    orders = jax.vmap(lambda subkey: jax.random.permutation(subkey, EXPERTS))(jax.random.split(key_perm, devices)).astype(jnp.int32)
    picked = jax.vmap(lambda subkey: jax.random.permutation(subkey, residues))(jax.random.split(key_order, devices)).astype(jnp.int32)
    hot_expert = jnp.repeat(jax.random.randint(key_hot, (GROUPS,), 0, EXPERTS, dtype=jnp.int32), devices // GROUPS)
    position_ids = jnp.arange(EXPERTS, dtype=jnp.int32)[None, :]
    where_hot = jnp.sum(jnp.where(orders == hot_expert[:, None], position_ids, 0), axis=1)
    first_pick = picked[:, 0]
    value_first = jnp.take_along_axis(orders, first_pick[:, None], axis=1)[:, 0]
    orders = jnp.where(position_ids == first_pick[:, None], hot_expert[:, None], jnp.where(position_ids == where_hot[:, None], value_first[:, None], orders))
    token_ids = jnp.arange(TOK_DEV, dtype=jnp.int32)
    residue = picked[:, token_ids % used_count]
    slot_places = residue[:, :, None] + jnp.arange(TOPK, dtype=jnp.int32)[None, None, :] * residues
    chosen = jnp.take_along_axis(orders, slot_places.reshape(devices, TOK_DEV * TOPK), axis=1)
    return chosen.reshape(TOKENS, TOPK).astype(jnp.int32)


def block_scale(rng, shape, cuts, least, top_value):
    level = 1.0
    for axis_at, shards_of in cuts:
        steps = jax.random.uniform(jax.random.fold_in(jax.random.fold_in(rng, 6), axis_at), (shards_of,), jnp.float32, least / len(cuts), top_value / len(cuts))
        level = level * jnp.repeat(jnp.exp(steps), shape[axis_at] // shards_of).reshape((-1,) + (1,) * (len(shape) - 1 - axis_at))
    return level


def gaussian(own_key, extent, spread, limit, pieces=(), held_as=jnp.bfloat16):
    loudness = block_scale(own_key, extent, pieces, -0.22, 0.18) if pieces else 1.0
    drawn = jax.random.normal(own_key, extent, jnp.float32) * spread * loudness
    return jnp.minimum(jnp.maximum(drawn, -limit), limit).astype(held_as)


def setup_inputs(seed: int = 0) -> dict:
    seeds = jax.random.split(jax.random.key(seed), 7)
    return {
        "out_grad": gaussian(seeds[0], (TOKENS, D), 1.0, 6.0, ((0, 1024),)),
        "routes": draw_routes(jax.random.fold_in(seeds[6], 71), 0),
        "gates": jnp.clip(jnp.exp(math.log(0.59765625) - 2.99491561 * jax.random.uniform(seeds[2], (TOKENS, TOPK), jnp.float32) ** block_scale(seeds[2], (TOKENS, TOPK), ((0, 1024),), -0.2, 0.2)), 0.029907227, 0.59765625).astype(jnp.bfloat16),
        "pre_gate": gaussian(seeds[3], (GROUPS, EXPERTS, SLOTS, FF), 1.0, 5.0, ((0, 8), (1, 128))),
        "pre_up": gaussian(seeds[4], (GROUPS, EXPERTS, SLOTS, FF), 1.0, 5.0, ((0, 8), (1, 128))),
        "down_weight": gaussian(seeds[5], (EXPERTS, FF, D), D ** -0.5, 0.125, ((0, 128),)),
    }


def reference(out_grad, routes, gates, pre_gate, pre_up, down_weight):
    token_ids = jnp.arange(TOKENS, dtype=jnp.int32)
    device = token_ids // TOK_DEV
    group_ids = device // EXPERTS
    source = device % EXPERTS
    expert_ids = jnp.arange(EXPERTS, dtype=jnp.int32)
    named_hits = (routes[:, :, None] == expert_ids[None, None, :]).astype(jnp.int32)
    hit_counts = jnp.sum(named_hits, axis=1).reshape(TOKENS // TOK_DEV, TOK_DEV, EXPERTS)
    before = (jnp.cumsum(hit_counts, axis=1) - hit_counts).reshape(TOKENS, EXPERTS)
    position = jnp.sum(named_hits * before[:, None, :], axis=2).astype(jnp.int32)
    slot_ids = source[:, None] * CAP + position
    flat_index = ((group_ids[:, None] * EXPERTS + routes) * SLOTS + slot_ids).reshape(-1).astype(jnp.int32)
    owners = jnp.broadcast_to(token_ids[:, None], (TOKENS, TOPK)).reshape(-1).astype(jnp.int32)
    slot_token = jnp.full((GROUPS * EXPERTS * SLOTS,), TOKENS, jnp.int32).at[flat_index].set(owners)
    slot_token = slot_token.reshape(GROUPS, EXPERTS, SLOTS)
    slot_gate = jnp.zeros((GROUPS * EXPERTS * SLOTS,), gates.dtype).at[flat_index].set(gates.reshape(-1))
    slot_gate = slot_gate.reshape(GROUPS, EXPERTS, SLOTS)
    padded = jnp.concatenate([out_grad, jnp.zeros((1, D), out_grad.dtype)], axis=0)

    def per_expert(expert):
        weight = down_weight[expert]
        total_grad = jnp.zeros((FF, D), jnp.float32)
        grads_gate = []
        grads_up = []
        slot_sums = []
        for group_index in range(GROUPS):
            routed_rows = padded[slot_token[group_index, expert]]
            gate_col = slot_gate[group_index, expert].astype(jnp.float32)
            gate_pre = pre_gate[group_index, expert].astype(jnp.float32)
            up_pre = pre_up[group_index, expert].astype(jnp.float32)
            sigmoid_a = jax.nn.sigmoid(gate_pre)
            hidden = (gate_pre * sigmoid_a * up_pre).astype(jnp.bfloat16)
            back_prop = lax.dot_general(routed_rows, weight, (((1,), (1,)), ((), ())),
                                        preferred_element_type=jnp.float32)
            slot_sums.append(jnp.sum(hidden.astype(jnp.float32) * back_prop, axis=1))
            carried = gate_col[:, None] * back_prop
            grads_gate.append((carried * up_pre * sigmoid_a * (1.0 + gate_pre * (1.0 - sigmoid_a))).astype(jnp.bfloat16))
            grads_up.append((carried * gate_pre * sigmoid_a).astype(jnp.bfloat16))
            scaled = (gate_col[:, None] * hidden.astype(jnp.float32)).astype(jnp.bfloat16)
            total_grad = total_grad + lax.dot_general(scaled, routed_rows, (((0,), (0,)), ((), ())),
                                                      preferred_element_type=jnp.float32)
        return (total_grad.astype(jnp.bfloat16), jnp.stack(grads_gate), jnp.stack(grads_up), jnp.stack(slot_sums))

    grad_down, grad_a, grad_b, slot_grad = lax.map(per_expert, expert_ids)
    grad_pre_gate = jnp.transpose(grad_a, (1, 0, 2, 3))
    grad_pre_up = jnp.transpose(grad_b, (1, 0, 2, 3))
    grad_gates = jnp.transpose(slot_grad, (1, 0, 2)).reshape(-1)[flat_index].reshape(TOKENS, TOPK)
    return grad_down, grad_pre_gate, grad_pre_up, grad_gates
```

```python
import functools

import jax
import jax.numpy as jnp
from jax import lax
from jax.experimental import pallas as pl
from jax.experimental.pallas import tpu as pltpu
from jax.sharding import PartitionSpec as P

MESH = pl.DeviceIdType.MESH
F32 = jnp.float32
BF16 = jnp.bfloat16
LANES = 128
SUBS = 4
AHEAD = 3
NT = (((1,), (1,)), ((), ()))


def iota(shape, dim):
    return lax.broadcasted_iota(jnp.int32, shape, dim)


def kernel(
    dims,
    grads_hbm, routes_ref, gates_ref, gate_hbm, up_hbm, weight_hbm,
    down_out, dgate_out, dup_out, droute_ref,
    gate_v, up_v, weight_v, tokens, table, routes_pad, gates_pad, place,
    hidden, factor_a, factor_b, gathered, tables, choose,
    rows_out, rows_in, gate_send, gate_rows, scaled_t, back_prop,
    part_out, part_in, part_sum, down_v, slot_out, slot_in, pack_out, pack_in,
    load_sem, token_sem, token_send, token_recv, table_send, table_recv,
    rows_send, rows_recv, gates_send, gates_recv, part_send, part_recv,
    slot_send, slot_recv, pack_send, pack_recv, store_sem,
):
    dp, wide, narrow, tok, top, feat, hid, slots = dims
    me_x, me_w, me_n = (lax.axis_index(a) for a in ("dp", "wide", "narrow"))
    right, left = lax.rem(me_x + 1, dp), lax.rem(me_x + dp - 1, dp)
    sub_rows = hid // SUBS
    blocks = hid // LANES

    def columns(step):
        first = lax.rem(me_x + (2 * dp - 1) - step, dp) * (2 * LANES)
        second = lax.rem(me_x + 1 + step, dp) * (2 * LANES) + LANES
        return pl.multiple_of(first, LANES), pl.multiple_of(second, LANES)

    def whole(ref, sem):
        pltpu.make_async_copy(ref, ref, sem).wait()

    for step in range(dp):
        for half, col in enumerate(columns(step)):
            pltpu.make_async_copy(
                grads_hbm.at[:, pl.ds(col, LANES)],
                tokens.at[step, pl.ds(half * tok, tok)],
                token_sem,
            ).start()
    loads = [
        pltpu.make_async_copy(src, dst, load_sem.at[k])
        for k, (src, dst) in enumerate(
            ((gate_hbm, gate_v), (up_hbm, up_v), (weight_hbm, weight_v))
        )
    ]
    for load in loads:
        load.start()

    barrier = pltpu.get_barrier_semaphore()
    for k in range(1, narrow):
        pl.semaphore_signal(
            barrier, inc=1, device_id={"narrow": lax.rem(me_n + k, narrow)}, device_id_type=MESH
        )
    for k in range(1, wide):
        pl.semaphore_signal(
            barrier, inc=1, device_id={"wide": lax.rem(me_w + k, wide)}, device_id_type=MESH
        )
    for peer in (right, left):
        pl.semaphore_signal(barrier, inc=1, device_id={"dp": peer}, device_id_type=MESH)

    routes_pad[...] = jnp.full((top, LANES), -1, jnp.int32)
    gates_pad[...] = jnp.zeros((top, LANES), F32)
    routes_pad[:, 0:tok] = routes_ref[...]
    gates_pad[:, 0:tok] = gates_ref[...].astype(F32)
    square = (LANES, LANES)
    expert_row = iota(square, 0)
    hits = jnp.zeros(square, F32)
    gate_at = jnp.zeros(square, F32)
    for k in range(top):
        same = routes_pad[k : k + 1, :] == expert_row
        hits = hits + jnp.where(same, 1.0, 0.0)
        gate_at = gate_at + jnp.where(same, gates_pad[k : k + 1, :], 0.0)
    earlier = jnp.where(iota(square, 0) < iota(square, 1), 1.0, 0.0).astype(BF16)
    before = jnp.dot(hits.astype(BF16), earlier, preferred_element_type=F32)
    for k in range(top):
        same = routes_pad[k : k + 1, :] == expert_row
        place[k : k + 1, :] = jnp.sum(jnp.where(same, before, 0.0), axis=0, keepdims=True)
    unit = jnp.where(iota((tok, LANES), 0) == iota((tok, LANES), 1), 1.0, 0.0).astype(BF16)
    for p in range(2):
        held = jnp.where(before == float(p), gate_at, 0.0).astype(BF16)
        table[:, p * LANES : (p + 1) * LANES] = lax.dot_general(
            unit, held, NT, preferred_element_type=F32
        ).astype(BF16)

    whole(tokens, token_sem)
    pl.semaphore_wait(barrier, (narrow - 1) + (wide - 1) + 2)

    def to_narrow(src, dst, send, recv):
        for k in range(1, narrow):
            pltpu.make_async_remote_copy(
                src_ref=src, dst_ref=dst.at[me_n], send_sem=send, recv_sem=recv,
                device_id={"narrow": lax.rem(me_n + k, narrow)}, device_id_type=MESH,
            ).start()
        pltpu.make_async_copy(src, dst.at[me_n], recv).start()

    def to_wide(src, dst, send, recv):
        for k in range(1, wide):
            peer = lax.rem(me_w + k, wide)
            pltpu.make_async_remote_copy(
                src_ref=src.at[peer], dst_ref=dst.at[me_w], send_sem=send, recv_sem=recv,
                device_id={"wide": peer}, device_id_type=MESH,
            ).start()
        pltpu.make_async_copy(src.at[me_w], dst.at[me_w], recv).start()

    def spread(step):
        to_narrow(tokens.at[step], gathered.at[step], token_send, token_recv.at[step])

    to_narrow(table, tables, table_send, table_recv)
    for step in range(AHEAD + 1):
        spread(step)

    for load in loads[:2]:
        load.wait()

    @pl.loop(0, blocks)
    def _(b):
        col = pl.ds(pl.multiple_of(b * LANES, LANES), LANES)
        gate = gate_v[:, col].astype(F32)
        up = up_v[:, col].astype(F32)
        sig = jax.nn.sigmoid(gate)
        silu = gate * sig
        hidden[:, col] = (silu * up).astype(BF16)
        factor_a[:, col] = up * sig * (1.0 + gate * (1.0 - sig))
        factor_b[:, col] = silu

    whole(tables, table_recv)
    pair = (slots, 2 * LANES)
    slot_row, entry = iota(pair, 0), iota(pair, 1)
    wanted = ((slot_row >> 4) * narrow + me_n) + (slot_row & 1) * LANES
    pick = jnp.where(entry == wanted, 1.0, 0.0).astype(BF16)
    full = lax.dot_general(
        pick, tables[...].reshape(narrow * tok, 2 * LANES), NT, preferred_element_type=F32
    )
    shape = (slots, narrow * tok)
    mine = ((iota(shape, 0) >> 1) & (narrow - 1)) == (iota(shape, 1) >> 4)
    gate_of = jnp.where(mine, full, 0.0)
    choose[...] = jnp.where(gate_of > 0.0, 1.0, 0.0).astype(BF16)
    gate_sum = jnp.sum(gate_of, axis=1, keepdims=True)
    gate_send[...] = (
        jnp.broadcast_to(gate_sum, (slots, LANES)).astype(BF16).reshape(wide, 2 * narrow, LANES)
    )
    to_wide(gate_send, gate_rows, gates_send, gates_recv)

    def forward(step):
        whole(gathered.at[step], token_recv.at[step])
        for half in range(2):
            held = gathered[step, :, half * tok : (half + 1) * tok, :].reshape(narrow * tok, LANES)
            picked = jnp.dot(choose[...], held, preferred_element_type=F32).astype(BF16)
            rows_out[step, :, half * tok : (half + 1) * tok, :] = picked.reshape(
                wide, 2 * narrow, LANES
            )
        to_wide(rows_out.at[step], rows_in.at[step], rows_send, rows_recv.at[step])

    forward(0)
    spread(AHEAD + 1)
    forward(1)
    spread(AHEAD + 2)

    whole(gate_rows, gates_recv)
    for b in range(blocks):
        col = slice(b * LANES, (b + 1) * LANES)
        gate = gate_rows[...].reshape(slots, LANES).astype(F32)
        scaled = (gate * hidden[:, col].astype(F32)).astype(BF16).astype(F32)
        scaled_t[b * LANES : (b + 1) * LANES, :] = scaled.T.astype(BF16)
    back_prop[...] = jnp.zeros_like(back_prop)

    forward(2)
    spread(AHEAD + 3)

    def rows(step, half):
        return rows_in[step, :, half * tok : (half + 1) * tok, :].reshape(slots, LANES)

    def arrive(step):
        whole(rows_in.at[step], rows_recv.at[step])

    def partial_of(step):
        for half in range(2):
            part_sum[half] = jnp.dot(scaled_t[...], rows(step, half), preferred_element_type=F32)

    def copy_of(step, half, sub, peer):
        at = pl.ds(sub * sub_rows, sub_rows)
        return pltpu.make_async_remote_copy(
            src_ref=part_out.at[step, half, at],
            dst_ref=part_in.at[step, half, at],
            send_sem=part_send,
            recv_sem=part_recv.at[step, half, sub],
            device_id={"dp": peer},
            device_id_type=MESH,
        )

    def ring(step, first):
        partial_of(step)
        for sub in range(SUBS):
            at = slice(sub * sub_rows, (sub + 1) * sub_rows)
            for half, peer in enumerate((right, left)):
                value = part_sum[half, at, :]
                if not first:
                    copy_of(step - 1, half, sub, peer).wait_recv()
                    value = value + part_in[step - 1, half, at, :].astype(F32)
                part_out[step, half, at, :] = value.astype(BF16)
                copy_of(step, half, sub, peer).start()

    def back(step):
        total = back_prop[...]
        for half, col in enumerate(columns(step)):
            total = total + lax.dot_general(
                rows(step, half), weight_v[:, pl.ds(col, LANES)], NT, preferred_element_type=F32
            )
        back_prop[...] = total

    arrive(0)
    ring(0, True)
    forward(3)
    spread(AHEAD + 4)
    loads[2].wait()
    back(0)

    @pl.loop(1, dp - AHEAD)
    def _(step):
        arrive(step)
        ring(step, False)
        forward(step + AHEAD)
        back(step)

    arrive(dp - 3)
    ring(dp - 3, False)
    back(dp - 3)
    for step in (dp - 2, dp - 1):
        arrive(step)
        back(step)

    dots = jnp.zeros((slots, LANES), F32)
    for b in range(blocks):
        col = slice(b * LANES, (b + 1) * LANES)
        bp = back_prop[:, col]
        gate = gate_rows[...].reshape(slots, LANES).astype(F32)
        carried = gate * bp
        dots = dots + hidden[:, col].astype(F32) * bp
        gate_v[:, col] = (carried * factor_a[:, col]).astype(BF16)
        up_v[:, col] = (carried * factor_b[:, col]).astype(BF16)
    sums = jnp.sum(dots, axis=1, keepdims=True)
    slot_out[...] = jnp.broadcast_to(sums, (slots, LANES)).reshape(wide, 2 * narrow, LANES)
    to_wide(slot_out, slot_in, slot_send, slot_recv)
    stores = [
        pltpu.make_async_copy(gate_v, dgate_out, store_sem.at[0]),
        pltpu.make_async_copy(up_v, dup_out, store_sem.at[1]),
    ]
    for store in stores:
        store.start()

    ring(dp - 2, False)

    whole(slot_in, slot_recv)
    flat = (2 * narrow, LANES)
    packed = jnp.zeros(flat, F32)
    for k in range(wide):
        packed = packed + jnp.where(iota(flat, 1) == me_n * wide + k, slot_in[k], 0.0)
    pack_out[...] = packed
    to_narrow(pack_out, pack_in, pack_send, pack_recv)

    partial_of(dp - 1)
    for sub in range(SUBS):
        at = slice(sub * sub_rows, (sub + 1) * sub_rows)
        for half, peer in enumerate((right, left)):
            copy_of(dp - 2, half, sub, peer).wait_recv()
            value = part_sum[half, at, :] + part_in[dp - 2, half, at, :].astype(F32)
            down_v[at, half * LANES : (half + 1) * LANES] = value.astype(BF16)
    last = pltpu.make_async_copy(down_v, down_out, store_sem.at[2])
    last.start()

    whole(pack_in, pack_recv)
    back_rows = jnp.sum(pack_in[...], axis=0)
    for k in range(top):
        named = routes_pad[k : k + 1, :]
        lane = (named & (narrow - 1)) * wide + (named >> 3)
        one = jnp.where(lane == iota(square, 0), 1.0, 0.0)
        got = jnp.dot(
            back_rows, one, precision=lax.Precision.HIGHEST, preferred_element_type=F32
        )
        row = 2 * me_n + place[k : k + 1, :].astype(jnp.int32)
        value = jnp.sum(jnp.where(iota(flat, 0) == row, got, 0.0), axis=0, keepdims=True)
        droute_ref[k : k + 1, :] = value[:, 0:tok]

    for store in stores:
        store.wait()
    last.wait()
    peers_n, peers_w = pl.ds(0, narrow - 1), pl.ds(0, wide - 1)
    for step in range(dp):
        whole(gathered.at[step, peers_n], token_send)
        whole(rows_in.at[step, peers_w], rows_send)
    whole(tables.at[peers_n], table_send)
    whole(gate_rows.at[peers_w], gates_send)
    whole(slot_in.at[peers_w], slot_send)
    whole(pack_in.at[peers_n], pack_send)
    whole(part_in, part_send)


def shards(out_grad, routes, gates, pre_gate, pre_up, down_weight):
    dp, wide, narrow = (lax.axis_size(a) for a in ("dp", "wide", "narrow"))
    tok, feat = out_grad.shape
    top = routes.shape[1]
    slots, hid = pre_gate.shape[2:]
    dims = (dp, wide, narrow, tok, top, feat, hid, slots)
    vmem, dma = pltpu.VMEM, pltpu.SemaphoreType.DMA
    any_spec = pl.BlockSpec(memory_space=pl.ANY)
    vmem_spec = pl.BlockSpec(memory_space=pltpu.VMEM)
    down, dgate, dup, droute = pl.pallas_call(
        functools.partial(kernel, dims),
        out_shape=(
            jax.ShapeDtypeStruct((hid, feat // dp), BF16),
            jax.ShapeDtypeStruct((slots, hid), BF16),
            jax.ShapeDtypeStruct((slots, hid), BF16),
            jax.ShapeDtypeStruct((top, tok), F32),
        ),
        in_specs=[any_spec, vmem_spec, vmem_spec, any_spec, any_spec, any_spec],
        out_specs=(any_spec, any_spec, any_spec, vmem_spec),
        scratch_shapes=[
            vmem((slots, hid), BF16),
            vmem((slots, hid), BF16),
            vmem((hid, feat), BF16),
            vmem((dp, 2 * tok, LANES), BF16),
            vmem((tok, 2 * LANES), BF16),
            vmem((top, LANES), jnp.int32),
            vmem((top, LANES), F32),
            vmem((top, LANES), F32),
            vmem((slots, hid), BF16),
            vmem((slots, hid), F32),
            vmem((slots, hid), F32),
            vmem((dp, narrow, 2 * tok, LANES), BF16),
            vmem((narrow, tok, 2 * LANES), BF16),
            vmem((slots, narrow * tok), BF16),
            vmem((dp, wide, 2 * tok, LANES), BF16),
            vmem((dp, wide, 2 * tok, LANES), BF16),
            vmem((wide, 2 * narrow, LANES), BF16),
            vmem((wide, 2 * narrow, LANES), BF16),
            vmem((hid, slots), BF16),
            vmem((slots, hid), F32),
            vmem((dp - 1, 2, hid, LANES), BF16),
            vmem((dp - 1, 2, hid, LANES), BF16),
            vmem((2, hid, LANES), F32),
            vmem((hid, 2 * LANES), BF16),
            vmem((wide, 2 * narrow, LANES), F32),
            vmem((wide, 2 * narrow, LANES), F32),
            vmem((2 * narrow, LANES), F32),
            vmem((narrow, 2 * narrow, LANES), F32),
            dma((3,)),
            dma,
            dma,
            dma((dp,)),
            dma,
            dma,
            dma,
            dma((dp,)),
            dma,
            dma,
            dma,
            dma((dp - 1, 2, SUBS)),
            dma,
            dma,
            dma,
            dma,
            dma((3,)),
        ],
        compiler_params=pltpu.CompilerParams(collective_id=0, has_side_effects=True),
        name="routed_backward",
    )(out_grad, routes.T, gates.T, pre_gate[0, 0], pre_up[0, 0], down_weight[0])
    return down[None], dgate[None, None], dup[None, None], droute.T


def solution(mesh):
    placed = (
        P(("dp", "wide", "narrow"), None),
        P(("dp", "wide", "narrow"), None),
        P(("dp", "wide", "narrow"), None),
        P("dp", ("wide", "narrow"), None, None),
        P("dp", ("wide", "narrow"), None, None),
        P(("wide", "narrow"), None, None),
    )
    return jax.shard_map(
        shards,
        mesh=mesh,
        in_specs=placed,
        out_specs=(
            P(("wide", "narrow"), None, "dp"),
            P("dp", ("wide", "narrow"), None, None),
            P("dp", ("wide", "narrow"), None, None),
            P(("dp", "wide", "narrow"), None),
        ),
        check_vma=False,
    )
```

```python
import functools

import jax
import jax.numpy as jnp
from jax import lax
from jax.experimental import pallas as pl
from jax.experimental.pallas import tpu as pltpu
from jax.sharding import PartitionSpec as P

MESH = pl.DeviceIdType.MESH
F32 = jnp.float32
BF16 = jnp.bfloat16
LANES = 128
SUBS = 4
AHEAD = 4
NT = (((1,), (1,)), ((), ()))


def iota(shape, dim):
    return lax.broadcasted_iota(jnp.int32, shape, dim)


def kernel(
    dims,
    grads_hbm, routes_hbm, gates_hbm, gate_hbm, up_hbm, weight_hbm,
    down_out, dgate_out, dup_out, droute_out,
    routes_v, gates_v, gate_v, up_v, weight_v, tokens, table, routes_pad, gates_pad, ranks, place,
    hidden, factor_a, factor_b, gathered, tables, choose,
    rows_out, rows_in, gate_send, gate_recv, gate_rows, scaled_t, back_prop,
    part_out, part_in, part_sum, down_v, droute_v, slot_out, slot_in, pack_out, pack_in,
    small_sem, load_sem, token_sem, token_send, token_recv, table_send, table_recv,
    rows_send, rows_recv, gates_send, gates_recv, part_send, part_recv,
    slot_send, slot_recv, pack_send, pack_recv, store_sem,
):
    dp, wide, narrow, tok, top, feat, hid, slots = dims
    me_x, me_w, me_n = (lax.axis_index(a) for a in ("dp", "wide", "narrow"))
    right, left = lax.rem(me_x + 1, dp), lax.rem(me_x + dp - 1, dp)
    sub_rows = hid // SUBS
    blocks = hid // LANES

    def columns(step):
        first = lax.rem(me_x + (2 * dp - 1) - step, dp) * (2 * LANES)
        second = lax.rem(me_x + 1 + step, dp) * (2 * LANES) + LANES
        return pl.multiple_of(first, LANES), pl.multiple_of(second, LANES)

    def whole(ref, sem):
        pltpu.make_async_copy(ref, ref, sem).wait()

    near = sorted(range(1, narrow), key=lambda k: -min(k, narrow - k))
    far = sorted(range(1, wide), key=lambda k: -min(k, wide - k))
    barrier = pltpu.get_barrier_semaphore()
    for k in near:
        pl.semaphore_signal(
            barrier, inc=1, device_id={"narrow": lax.rem(me_n + k, narrow)}, device_id_type=MESH
        )
    for k in far:
        pl.semaphore_signal(
            barrier, inc=1, device_id={"wide": lax.rem(me_w + k, wide)}, device_id_type=MESH
        )
    for peer in (right, left):
        pl.semaphore_signal(barrier, inc=1, device_id={"dp": peer}, device_id_type=MESH)

    small = [
        pltpu.make_async_copy(src, dst, small_sem.at[k])
        for k, (src, dst) in enumerate(((routes_hbm, routes_v), (gates_hbm, gates_v)))
    ]
    for load in small:
        load.start()
    for step in range(dp):
        for half, col in enumerate(columns(step)):
            pltpu.make_async_copy(
                grads_hbm.at[:, pl.ds(col, LANES)],
                tokens.at[step, pl.ds(half * tok, tok)],
                token_sem,
            ).start()
    loads = [
        pltpu.make_async_copy(src, dst, load_sem.at[k])
        for k, (src, dst) in enumerate(
            ((gate_hbm, gate_v), (up_hbm, up_v), (weight_hbm, weight_v))
        )
    ]

    routes_pad[...] = jnp.full((top, LANES), -1, jnp.int32)
    gates_pad[...] = jnp.zeros((top, LANES), F32)
    for load in small:
        load.wait()
    routes_pad[:, 0:tok] = routes_v[...]
    gates_pad[:, 0:tok] = gates_v[...].astype(F32)
    square = (LANES, LANES)
    expert_row = iota(square, 0)
    hits = jnp.zeros(square, F32)
    gate_at = jnp.zeros(square, F32)
    for k in range(top):
        same = routes_pad[k : k + 1, :] == expert_row
        hits = jnp.where(same, 1.0, hits)
        gate_at = jnp.where(same, gates_pad[k : k + 1, :], gate_at)
    earlier = jnp.where(iota(square, 0) < iota(square, 1), 1.0, 0.0).astype(BF16)
    before = jnp.dot(hits.astype(BF16), earlier, preferred_element_type=F32)
    ranks[...] = before
    unit = jnp.where(iota((tok, LANES), 0) == iota((tok, LANES), 1), 1.0, 0.0).astype(BF16)
    held = jnp.where(before == 0.0, gate_at, jnp.where(before == 1.0, -gate_at, 0.0)).astype(BF16)
    table[...] = lax.dot_general(unit, held, NT, preferred_element_type=F32).astype(BF16)

    pl.semaphore_wait(barrier, (narrow - 1) + (wide - 1) + 2)

    def to_narrow(src, dst, send, recv):
        for k in near:
            pltpu.make_async_remote_copy(
                src_ref=src, dst_ref=dst.at[me_n], send_sem=send, recv_sem=recv,
                device_id={"narrow": lax.rem(me_n + k, narrow)}, device_id_type=MESH,
            ).start()
        pltpu.make_async_copy(src, dst.at[me_n], recv).start()

    def to_wide(src, dst, send, recv):
        for k in far:
            peer = lax.rem(me_w + k, wide)
            pltpu.make_async_remote_copy(
                src_ref=src.at[peer], dst_ref=dst.at[me_w], send_sem=send, recv_sem=recv,
                device_id={"wide": peer}, device_id_type=MESH,
            ).start()
        pltpu.make_async_copy(src.at[me_w], dst.at[me_w], recv).start()

    def spread(step):
        to_narrow(tokens.at[step], gathered.at[step], token_send, token_recv.at[step])

    to_narrow(table, tables, table_send, table_recv)
    whole(tokens, token_sem)
    for step in range(AHEAD):
        spread(step)
    for load in loads:
        load.start()

    for k in range(top):
        same = routes_pad[k : k + 1, :] == expert_row
        place[k : k + 1, :] = jnp.sum(jnp.where(same, ranks[...], 0.0), axis=0, keepdims=True)
    for load in loads[:2]:
        load.wait()

    @pl.loop(0, blocks)
    def _(b):
        col = pl.ds(pl.multiple_of(b * LANES, LANES), LANES)
        gate = gate_v[:, col].astype(F32)
        up = up_v[:, col].astype(F32)
        sig = jax.nn.sigmoid(gate)
        silu = gate * sig
        hidden[:, col] = (silu * up).astype(BF16)
        factor_a[:, col] = up * sig * (1.0 + gate * (1.0 - sig))
        factor_b[:, col] = silu

    whole(tables, table_recv)
    shape = (slots, narrow * tok)
    slot_row, entry = iota(shape, 0), iota(shape, 1)
    pick = jnp.where(entry == (slot_row >> 4) * narrow + me_n, 1.0, 0.0).astype(BF16)
    full = lax.dot_general(
        pick, tables[...].reshape(narrow * tok, LANES), NT, preferred_element_type=F32
    )
    mine = ((slot_row >> 1) & (narrow - 1)) == (entry >> 4)
    signed = jnp.where((slot_row & 1) == 0, full, -full)
    gate_of = jnp.where(mine, jnp.maximum(signed, 0.0), 0.0)
    choose[...] = jnp.where(gate_of > 0.0, 1.0, 0.0).astype(BF16)

    cube = (wide, 2 * narrow, LANES)
    diagonal = iota(cube, 1) == iota(cube, 2)

    def to_lanes(column):
        spread_out = jnp.broadcast_to(column, (slots, LANES)).reshape(cube)
        return jnp.sum(jnp.where(diagonal, spread_out, 0.0), axis=1, keepdims=True)

    def to_rows(lanes):
        spread_out = jnp.where(diagonal, jnp.broadcast_to(lanes, cube), 0.0)
        return jnp.broadcast_to(jnp.sum(spread_out, axis=2, keepdims=True), cube)

    gate_send[...] = to_lanes(jnp.sum(gate_of, axis=1, keepdims=True))
    to_wide(gate_send, gate_recv, gates_send, gates_recv)

    def forward(step):
        whole(gathered.at[step], token_recv.at[step])
        for half in range(2):
            held = gathered[step, :, half * tok : (half + 1) * tok, :].reshape(narrow * tok, LANES)
            picked = jnp.dot(choose[...], held, preferred_element_type=F32).astype(BF16)
            rows_out[step, :, half * tok : (half + 1) * tok, :] = picked.reshape(
                wide, 2 * narrow, LANES
            )
        to_wide(rows_out.at[step], rows_in.at[step], rows_send, rows_recv.at[step])

    forward(0)
    spread(AHEAD)
    forward(1)
    spread(AHEAD + 1)

    whole(gate_recv, gates_recv)
    gate_rows[...] = to_rows(gate_recv[...]).reshape(slots, LANES)
    for b in range(blocks):
        col = slice(b * LANES, (b + 1) * LANES)
        scaled = (gate_rows[...] * hidden[:, col].astype(F32)).astype(BF16).astype(F32)
        scaled_t[b * LANES : (b + 1) * LANES, :] = scaled.T.astype(BF16)
    back_prop[...] = jnp.zeros_like(back_prop)

    forward(2)
    spread(AHEAD + 2)
    forward(3)
    spread(AHEAD + 3)

    def rows(step, half):
        return rows_in[step, :, half * tok : (half + 1) * tok, :].reshape(slots, LANES)

    def arrive(step):
        whole(rows_in.at[step], rows_recv.at[step])

    def partial_of(step):
        for half in range(2):
            part_sum[half] = jnp.dot(scaled_t[...], rows(step, half), preferred_element_type=F32)

    def copy_of(step, half, sub, peer):
        at = pl.ds(sub * sub_rows, sub_rows)
        return pltpu.make_async_remote_copy(
            src_ref=part_out.at[step, half, at],
            dst_ref=part_in.at[step, half, at],
            send_sem=part_send,
            recv_sem=part_recv.at[step, half, sub],
            device_id={"dp": peer},
            device_id_type=MESH,
        )

    def ring(step, first, between=None):
        partial_of(step)
        for sub in range(SUBS):
            if sub == SUBS // 2 and between is not None:
                between()
            at = slice(sub * sub_rows, (sub + 1) * sub_rows)
            for half, peer in enumerate((right, left)):
                value = part_sum[half, at, :]
                if not first:
                    copy_of(step - 1, half, sub, peer).wait_recv()
                    value = value + part_in[step - 1, half, at, :].astype(F32)
                part_out[step, half, at, :] = value.astype(BF16)
                copy_of(step, half, sub, peer).start()

    def back(step):
        total = back_prop[...]
        for half, col in enumerate(columns(step)):
            total = total + lax.dot_general(
                rows(step, half), weight_v[:, pl.ds(col, LANES)], NT, preferred_element_type=F32
            )
        back_prop[...] = total

    arrive(0)
    ring(0, True)
    forward(AHEAD)
    loads[2].wait()
    back(0)

    @pl.loop(1, dp - AHEAD)
    def _(step):
        arrive(step)
        ring(step, False)
        forward(step + AHEAD)
        back(step)

    @pl.loop(dp - AHEAD, dp - 3)
    def _(step):
        arrive(step)
        ring(step, False)
        back(step)

    stores = [
        pltpu.make_async_copy(gate_v, dgate_out, store_sem.at[0]),
        pltpu.make_async_copy(up_v, dup_out, store_sem.at[1]),
    ]

    def finish():
        back(dp - 3)
        for step in (dp - 2, dp - 1):
            arrive(step)
            back(step)
        dots = jnp.zeros((slots, LANES), F32)
        for b in range(blocks):
            col = slice(b * LANES, (b + 1) * LANES)
            dots = dots + hidden[:, col].astype(F32) * back_prop[:, col]
        slot_out[...] = to_lanes(jnp.sum(dots, axis=1, keepdims=True))
        to_wide(slot_out, slot_in, slot_send, slot_recv)

    arrive(dp - 3)
    ring(dp - 3, False, finish)
    for b in range(blocks):
        col = slice(b * LANES, (b + 1) * LANES)
        carried = gate_rows[...] * back_prop[:, col]
        gate_v[:, col] = (carried * factor_a[:, col]).astype(BF16)
        up_v[:, col] = (carried * factor_b[:, col]).astype(BF16)
    for store in stores:
        store.start()
    ring(dp - 2, False)

    whole(slot_in, slot_recv)
    here = iota(cube, 2) == me_n * wide + iota(cube, 0)
    packed = jnp.sum(jnp.where(here, to_rows(slot_in[...]), 0.0), axis=0)
    for k in range(2 * narrow):
        pack_out[k // 2, k % 2 : k % 2 + 1, :] = packed[k : k + 1, :]
    for k in near:
        peer = lax.rem(me_n + k, narrow)
        pltpu.make_async_remote_copy(
            src_ref=pack_out.at[peer], dst_ref=pack_in.at[me_n],
            send_sem=pack_send, recv_sem=pack_recv,
            device_id={"narrow": peer}, device_id_type=MESH,
        ).start()
    pltpu.make_async_copy(pack_out.at[me_n], pack_in.at[me_n], pack_recv).start()

    partial_of(dp - 1)
    for sub in range(SUBS):
        at = slice(sub * sub_rows, (sub + 1) * sub_rows)
        for half, peer in enumerate((right, left)):
            copy_of(dp - 2, half, sub, peer).wait_recv()
            value = part_sum[half, at, :] + part_in[dp - 2, half, at, :].astype(F32)
            down_v[at, half * LANES : (half + 1) * LANES] = value.astype(BF16)
    last = pltpu.make_async_copy(down_v, down_out, store_sem.at[2])
    last.start()

    whole(pack_in, pack_recv)
    back_rows = jnp.sum(pack_in[...], axis=0)
    for k in range(top):
        named = routes_pad[k : k + 1, :]
        lane = (named & (narrow - 1)) * wide + (named >> 3)
        one = jnp.where(lane == expert_row, 1.0, 0.0)
        got = jnp.dot(
            back_rows, one, precision=lax.Precision.HIGHEST, preferred_element_type=F32
        )
        value = jnp.where(place[k : k + 1, :] == 0.0, got[0:1, :], got[1:2, :])
        droute_v[k : k + 1, :] = value[:, 0:tok]
    routed = pltpu.make_async_copy(droute_v, droute_out, store_sem.at[3])
    routed.start()

    for store in stores:
        store.wait()
    last.wait()
    routed.wait()
    peers_n, peers_w = pl.ds(0, narrow - 1), pl.ds(0, wide - 1)
    for step in range(dp):
        whole(gathered.at[step, peers_n], token_send)
        whole(rows_in.at[step, peers_w], rows_send)
    whole(tables.at[peers_n], table_send)
    whole(gate_recv.at[peers_w], gates_send)
    whole(slot_in.at[peers_w], slot_send)
    whole(pack_in.at[peers_n], pack_send)
    whole(part_in, part_send)


def hand_on(*refs):
    sources, targets, held = refs[0:4], refs[4:8], refs[8:12]
    taken, given = refs[12:]
    reads = [pltpu.make_async_copy(a, b, taken.at[k]) for k, (a, b) in enumerate(zip(sources, held))]
    writes = [pltpu.make_async_copy(a, b, given.at[k]) for k, (a, b) in enumerate(zip(held, targets))]
    for read in reads:
        read.start()
    for read, write in zip(reads, writes):
        read.wait()
        write.start()
    for write in writes:
        write.wait()


def shards(out_grad, routes, gates, pre_gate, pre_up, down_weight):
    dp, wide, narrow = (lax.axis_size(a) for a in ("dp", "wide", "narrow"))
    tok, feat = out_grad.shape
    top = routes.shape[1]
    slots, hid = pre_gate.shape[2:]
    dims = (dp, wide, narrow, tok, top, feat, hid, slots)
    vmem, dma = pltpu.VMEM, pltpu.SemaphoreType.DMA
    any_spec = pl.BlockSpec(memory_space=pl.ANY)
    made = pl.pallas_call(
        functools.partial(kernel, dims),
        out_shape=(
            jax.ShapeDtypeStruct((hid, feat // dp), BF16),
            jax.ShapeDtypeStruct((slots, hid), BF16),
            jax.ShapeDtypeStruct((slots, hid), BF16),
            jax.ShapeDtypeStruct((top, tok), F32),
        ),
        in_specs=[any_spec] * 6,
        out_specs=(any_spec,) * 4,
        scratch_shapes=[
            vmem((top, tok), jnp.int32),
            vmem((top, tok), BF16),
            vmem((slots, hid), BF16),
            vmem((slots, hid), BF16),
            vmem((hid, feat), BF16),
            vmem((dp, 2 * tok, LANES), BF16),
            vmem((tok, LANES), BF16),
            vmem((top, LANES), jnp.int32),
            vmem((top, LANES), F32),
            vmem((LANES, LANES), F32),
            vmem((top, LANES), F32),
            vmem((slots, hid), BF16),
            vmem((slots, hid), F32),
            vmem((slots, hid), F32),
            vmem((dp, narrow, 2 * tok, LANES), BF16),
            vmem((narrow, tok, LANES), BF16),
            vmem((slots, narrow * tok), BF16),
            vmem((dp, wide, 2 * tok, LANES), BF16),
            vmem((dp, wide, 2 * tok, LANES), BF16),
            vmem((wide, 1, LANES), F32),
            vmem((wide, 1, LANES), F32),
            vmem((slots, LANES), F32),
            vmem((hid, slots), BF16),
            vmem((slots, hid), F32),
            vmem((dp - 1, 2, hid, LANES), BF16),
            vmem((dp - 1, 2, hid, LANES), BF16),
            vmem((2, hid, LANES), F32),
            vmem((hid, 2 * LANES), BF16),
            vmem((top, tok), F32),
            vmem((wide, 1, LANES), F32),
            vmem((wide, 1, LANES), F32),
            vmem((narrow, 2, LANES), F32),
            vmem((narrow, 2, LANES), F32),
            dma((2,)),
            dma((3,)),
            dma,
            dma,
            dma((dp,)),
            dma,
            dma,
            dma,
            dma((dp,)),
            dma,
            dma,
            dma,
            dma((dp - 1, 2, SUBS)),
            dma,
            dma,
            dma,
            dma,
            dma((4,)),
        ],
        compiler_params=pltpu.CompilerParams(collective_id=0, has_side_effects=True),
        name="routed_backward",
    )(out_grad, routes.T, gates.T, pre_gate[0, 0], pre_up[0, 0], down_weight[0])
    down, dgate, dup, droute = pl.pallas_call(
        hand_on,
        out_shape=tuple(jax.ShapeDtypeStruct(a.shape, a.dtype) for a in made),
        in_specs=[any_spec] * 4,
        out_specs=(any_spec,) * 4,
        scratch_shapes=[vmem(a.shape, a.dtype) for a in made] + [dma((4,)), dma((4,))],
        name="hand_on",
    )(*made)
    return down[None], dgate[None, None], dup[None, None], droute.T


def solution(mesh):
    placed = (
        P(("dp", "wide", "narrow"), None),
        P(("dp", "wide", "narrow"), None),
        P(("dp", "wide", "narrow"), None),
        P("dp", ("wide", "narrow"), None, None),
        P("dp", ("wide", "narrow"), None, None),
        P(("wide", "narrow"), None, None),
    )
    return jax.shard_map(
        shards,
        mesh=mesh,
        in_specs=placed,
        out_specs=(
            P(("wide", "narrow"), None, "dp"),
            P("dp", ("wide", "narrow"), None, None),
            P("dp", ("wide", "narrow"), None, None),
            P(("dp", "wide", "narrow"), None),
        ),
        check_vma=False,
    )
```

```python
import functools

import jax
import jax.numpy as jnp
from jax import lax
from jax.experimental import pallas as pl
from jax.experimental.pallas import tpu as pltpu
from jax.sharding import PartitionSpec as P

MESH = pl.DeviceIdType.MESH
F32 = jnp.float32
BF16 = jnp.bfloat16
LANES = 128
SUBS = 4
FINISH = 1
NT = (((1,), (1,)), ((), ()))


def iota(shape, dim):
    return lax.broadcasted_iota(jnp.int32, shape, dim)


def kernel(
    dims,
    grads_hbm, routes_hbm, gates_hbm, gate_hbm, up_hbm, weight_hbm,
    down_out, dgate_out, dup_out, pack_res, place_out,
    routes_v, gates_v, gate_v, up_v, weight_v, tokens, table, routes_pad, gates_pad, ranks, place,
    hidden, factor_a, factor_b, gathered, tables, choose,
    rows_out, rows_in, gate_send, gate_recv, gate_rows, scaled_t, back_prop,
    part_out, part_in, part_sum, down_v, slot_out, slot_in, pack_out, pack_in,
    small_sem, load_sem, token_sem, token_send, token_recv, table_send, table_recv,
    rows_send, rows_recv, gates_send, gates_recv, part_send, part_recv,
    slot_send, slot_recv, pack_send, pack_recv, store_sem, down_sem,
):
    dp, wide, narrow, tok, top, feat, hid, slots = dims
    me_x, me_w, me_n = (lax.axis_index(a) for a in ("dp", "wide", "narrow"))
    right, left = lax.rem(me_x + 1, dp), lax.rem(me_x + dp - 1, dp)
    sub_rows = hid // SUBS
    blocks = hid // LANES

    def columns(step):
        first = lax.rem(me_x + (2 * dp - 1) - step, dp) * (2 * LANES)
        second = lax.rem(me_x + 1 + step, dp) * (2 * LANES) + LANES
        return pl.multiple_of(first, LANES), pl.multiple_of(second, LANES)

    def whole(ref, sem):
        pltpu.make_async_copy(ref, ref, sem).wait()

    small = [
        pltpu.make_async_copy(src, dst, small_sem.at[k])
        for k, (src, dst) in enumerate(((routes_hbm, routes_v), (gates_hbm, gates_v)))
    ]
    for load in small:
        load.start()

    near = sorted(range(1, narrow), key=lambda k: -min(k, narrow - k))
    far = sorted(range(1, wide), key=lambda k: -min(k, wide - k))
    barrier = pltpu.get_barrier_semaphore()
    for k in near:
        pl.semaphore_signal(
            barrier, inc=1, device_id={"narrow": lax.rem(me_n + k, narrow)}, device_id_type=MESH
        )
    for k in far:
        pl.semaphore_signal(
            barrier, inc=1, device_id={"wide": lax.rem(me_w + k, wide)}, device_id_type=MESH
        )
    for peer in (right, left):
        pl.semaphore_signal(barrier, inc=1, device_id={"dp": peer}, device_id_type=MESH)

    for step in range(dp):
        for half, col in enumerate(columns(step)):
            pltpu.make_async_copy(
                grads_hbm.at[:, pl.ds(col, LANES)],
                tokens.at[step, pl.ds(half * tok, tok)],
                token_sem,
            ).start()
    loads = [
        pltpu.make_async_copy(src, dst, load_sem.at[k])
        for k, (src, dst) in enumerate(
            ((gate_hbm, gate_v), (up_hbm, up_v), (weight_hbm, weight_v))
        )
    ]

    routes_pad[...] = jnp.full((top, LANES), -1, jnp.int32)
    gates_pad[...] = jnp.zeros((top, LANES), F32)
    for load in small:
        load.wait()
    routes_pad[:, 0:tok] = routes_v[...]
    gates_pad[:, 0:tok] = gates_v[...].astype(F32)
    square = (LANES, LANES)
    expert_row = iota(square, 0)
    hits = jnp.zeros(square, F32)
    gate_at = jnp.zeros(square, F32)
    for k in range(top):
        same = routes_pad[k : k + 1, :] == expert_row
        hits = jnp.where(same, 1.0, hits)
        gate_at = jnp.where(same, gates_pad[k : k + 1, :], gate_at)
    earlier = jnp.where(iota(square, 0) < iota(square, 1), 1.0, 0.0).astype(BF16)
    before = jnp.dot(hits.astype(BF16), earlier, preferred_element_type=F32)
    ranks[...] = before
    unit = jnp.where(iota((tok, LANES), 0) == iota((tok, LANES), 1), 1.0, 0.0).astype(BF16)
    held = jnp.where(before == 0.0, gate_at, jnp.where(before == 1.0, -gate_at, 0.0)).astype(BF16)
    table[...] = lax.dot_general(unit, held, NT, preferred_element_type=F32).astype(BF16)

    pl.semaphore_wait(barrier, (narrow - 1) + (wide - 1) + 2)

    def to_narrow(src, dst, send, recv):
        for k in near:
            pltpu.make_async_remote_copy(
                src_ref=src, dst_ref=dst.at[me_n], send_sem=send, recv_sem=recv,
                device_id={"narrow": lax.rem(me_n + k, narrow)}, device_id_type=MESH,
            ).start()
        pltpu.make_async_copy(src, dst.at[me_n], recv).start()

    def to_wide(src, dst, send, recv):
        for k in far:
            peer = lax.rem(me_w + k, wide)
            pltpu.make_async_remote_copy(
                src_ref=src.at[peer], dst_ref=dst.at[me_w], send_sem=send, recv_sem=recv,
                device_id={"wide": peer}, device_id_type=MESH,
            ).start()
        pltpu.make_async_copy(src.at[me_w], dst.at[me_w], recv).start()

    def spread(step):
        to_narrow(tokens.at[step], gathered.at[step], token_send, token_recv.at[step])

    to_narrow(table, tables, table_send, table_recv)
    whole(tokens, token_sem)
    for step in range(4):
        spread(step)
    for load in loads:
        load.start()

    whole(tables, table_recv)
    shape = (slots, narrow * tok)
    slot_row, entry = iota(shape, 0), iota(shape, 1)
    pick = jnp.where(entry == (slot_row >> 4) * narrow + me_n, 1.0, 0.0).astype(BF16)
    full = lax.dot_general(
        pick, tables[...].reshape(narrow * tok, LANES), NT, preferred_element_type=F32
    )
    mine = ((slot_row >> 1) & (narrow - 1)) == (entry >> 4)
    signed = jnp.where((slot_row & 1) == 0, full, -full)
    gate_of = jnp.where(mine, jnp.maximum(signed, 0.0), 0.0)
    choose[...] = jnp.where(gate_of > 0.0, 1.0, 0.0).astype(BF16)

    cube = (wide, 2 * narrow, LANES)
    diagonal = iota(cube, 1) == iota(cube, 2)

    def to_lanes(column):
        spread_out = jnp.broadcast_to(column, (slots, LANES)).reshape(cube)
        return jnp.sum(jnp.where(diagonal, spread_out, 0.0), axis=1, keepdims=True)

    def to_rows(lanes):
        spread_out = jnp.where(diagonal, jnp.broadcast_to(lanes, cube), 0.0)
        return jnp.broadcast_to(jnp.sum(spread_out, axis=2, keepdims=True), cube)

    gate_send[...] = to_lanes(jnp.sum(gate_of, axis=1, keepdims=True))
    to_wide(gate_send, gate_recv, gates_send, gates_recv)

    def forward(step):
        whole(gathered.at[step], token_recv.at[step])
        for half in range(2):
            held = gathered[step, :, half * tok : (half + 1) * tok, :].reshape(narrow * tok, LANES)
            picked = jnp.dot(choose[...], held, preferred_element_type=F32).astype(BF16)
            rows_out[step, :, half * tok : (half + 1) * tok, :] = picked.reshape(
                wide, 2 * narrow, LANES
            )
        to_wide(rows_out.at[step], rows_in.at[step], rows_send, rows_recv.at[step])

    forward(0)
    spread(4)
    spread(5)

    for k in range(top):
        same = routes_pad[k : k + 1, :] == expert_row
        place[k : k + 1, :] = jnp.sum(jnp.where(same, ranks[...], 0.0), axis=0, keepdims=True)
    for load in loads[:2]:
        load.wait()

    @pl.loop(0, blocks)
    def _(b):
        col = pl.ds(pl.multiple_of(b * LANES, LANES), LANES)
        gate = gate_v[:, col].astype(F32)
        up = up_v[:, col].astype(F32)
        sig = jax.nn.sigmoid(gate)
        silu = gate * sig
        hidden[:, col] = (silu * up).astype(BF16)
        factor_a[:, col] = up * sig * (1.0 + gate * (1.0 - sig))
        factor_b[:, col] = silu

    forward(1)
    spread(6)
    spread(7)

    whole(gate_recv, gates_recv)
    gate_rows[...] = to_rows(gate_recv[...]).reshape(slots, LANES)
    for b in range(blocks):
        col = slice(b * LANES, (b + 1) * LANES)
        scaled = (gate_rows[...] * hidden[:, col].astype(F32)).astype(BF16).astype(F32)
        scaled_t[b * LANES : (b + 1) * LANES, :] = scaled.T.astype(BF16)
    back_prop[...] = jnp.zeros_like(back_prop)

    def rows(step, half):
        return rows_in[step, :, half * tok : (half + 1) * tok, :].reshape(slots, LANES)

    def arrive(step):
        whole(rows_in.at[step], rows_recv.at[step])

    def partial_of(step):
        for half in range(2):
            part_sum[half] = jnp.dot(scaled_t[...], rows(step, half), preferred_element_type=F32)

    def copy_of(step, half, sub, peer):
        at = pl.ds(sub * sub_rows, sub_rows)
        return pltpu.make_async_remote_copy(
            src_ref=part_out.at[step, half, at],
            dst_ref=part_in.at[step, half, at],
            send_sem=part_send,
            recv_sem=part_recv.at[step, half, sub],
            device_id={"dp": peer},
            device_id_type=MESH,
        )

    def ring(step, first, between=None, when=0):
        partial_of(step)
        for sub in range(SUBS):
            if sub == when and between is not None:
                between()
            at = slice(sub * sub_rows, (sub + 1) * sub_rows)
            for half, peer in enumerate((right, left)):
                value = part_sum[half, at, :]
                if not first:
                    copy_of(step - 1, half, sub, peer).wait_recv()
                    value = value + part_in[step - 1, half, at, :].astype(F32)
                part_out[step, half, at, :] = value.astype(BF16)
                copy_of(step, half, sub, peer).start()

    def back(step):
        total = back_prop[...]
        for half, col in enumerate(columns(step)):
            total = total + lax.dot_general(
                rows(step, half), weight_v[:, pl.ds(col, LANES)], NT, preferred_element_type=F32
            )
        back_prop[...] = total

    arrive(0)
    forward(2)
    ring(0, True)
    pl.loop(3, 5)(forward)
    loads[2].wait()
    back(0)

    @pl.loop(1, 3)
    def _(step):
        arrive(step)
        ring(step, False)
        pl.loop(2 * step + 3, jnp.minimum(2 * step + 5, dp))(forward)
        back(step)

    @pl.loop(3, dp - 3)
    def _(step):
        arrive(step)
        ring(step, False)
        back(step)

    stores = [
        pltpu.make_async_copy(gate_v, dgate_out, store_sem.at[0]),
        pltpu.make_async_copy(up_v, dup_out, store_sem.at[1]),
    ]

    def finish():
        back(dp - 3)
        for step in (dp - 2, dp - 1):
            arrive(step)
            back(step)
        dots = jnp.zeros((slots, LANES), F32)
        for b in range(blocks):
            col = slice(b * LANES, (b + 1) * LANES)
            dots = dots + hidden[:, col].astype(F32) * back_prop[:, col]
        slot_out[...] = to_lanes(jnp.sum(dots, axis=1, keepdims=True))
        to_wide(slot_out, slot_in, slot_send, slot_recv)

    arrive(dp - 3)
    ring(dp - 3, False, finish, FINISH)
    for b in range(blocks):
        col = slice(b * LANES, (b + 1) * LANES)
        carried = gate_rows[...] * back_prop[:, col]
        gate_v[:, col] = (carried * factor_a[:, col]).astype(BF16)
        up_v[:, col] = (carried * factor_b[:, col]).astype(BF16)
    for store in stores:
        store.start()
    placed_out = pltpu.make_async_copy(place, place_out, store_sem.at[2])
    placed_out.start()
    ring(dp - 2, False)

    whole(slot_in, slot_recv)
    here = iota(cube, 2) == me_n * wide + iota(cube, 0)
    packed = jnp.sum(jnp.where(here, to_rows(slot_in[...]), 0.0), axis=0)
    for k in range(2 * narrow):
        pack_out[k // 2, k % 2 : k % 2 + 1, :] = packed[k : k + 1, :]
    for k in near:
        peer = lax.rem(me_n + k, narrow)
        pltpu.make_async_remote_copy(
            src_ref=pack_out.at[peer], dst_ref=pack_in.at[me_n],
            send_sem=pack_send, recv_sem=pack_recv,
            device_id={"narrow": peer}, device_id_type=MESH,
        ).start()
    pltpu.make_async_copy(pack_out.at[me_n], pack_in.at[me_n], pack_recv).start()

    downs = []
    partial_of(dp - 1)
    for sub in range(SUBS):
        at = slice(sub * sub_rows, (sub + 1) * sub_rows)
        for half, peer in enumerate((right, left)):
            copy_of(dp - 2, half, sub, peer).wait_recv()
            value = part_sum[half, at, :] + part_in[dp - 2, half, at, :].astype(F32)
            down_v[at, half * LANES : (half + 1) * LANES] = value.astype(BF16)
        sends = pltpu.make_async_copy(
            down_v.at[pl.ds(sub * sub_rows, sub_rows)],
            down_out.at[pl.ds(sub * sub_rows, sub_rows)],
            down_sem.at[sub],
        )
        sends.start()
        downs.append(sends)

    whole(pack_in, pack_recv)
    packs = pltpu.make_async_copy(pack_in, pack_res, store_sem.at[3])
    packs.start()

    for store in stores:
        store.wait()
    placed_out.wait()
    packs.wait()
    for send in downs:
        send.wait()
    peers_n, peers_w = pl.ds(0, narrow - 1), pl.ds(0, wide - 1)
    for step in range(dp):
        whole(gathered.at[step, peers_n], token_send)
        whole(rows_in.at[step, peers_w], rows_send)
    whole(tables.at[peers_n], table_send)
    whole(gate_recv.at[peers_w], gates_send)
    whole(slot_in.at[peers_w], slot_send)
    whole(pack_in.at[peers_n], pack_send)
    whole(part_in, part_send)


def hand_on(wide, narrow, *refs):
    sources, small, targets, route_out = refs[0:3], refs[3:6], refs[6:9], refs[9]
    held, result, taken, given = refs[10:13], refs[13], refs[14], refs[15]
    pack, place, routes = held
    writes = [
        pltpu.make_async_copy(a, b, given.at[k])
        for k, (a, b) in enumerate([*zip(sources, targets), (result, route_out)])
    ]
    reads = [pltpu.make_async_copy(a, b, taken.at[k]) for k, (a, b) in enumerate(zip(small, held))]
    for copy in reads + writes[:3]:
        copy.start()
    for read in reads:
        read.wait()
    top, tok = result.shape
    rows = jnp.sum(pack[...], axis=0)
    for k in range(top):
        named = routes[k : k + 1, :]
        lane = (named & (narrow - 1)) * wide + (named >> 3)
        one = jnp.where(lane == iota((LANES, tok), 0), 1.0, 0.0)
        got = jnp.dot(rows, one, precision=lax.Precision.HIGHEST, preferred_element_type=F32)
        result[k : k + 1, :] = jnp.where(place[k : k + 1, 0:tok] == 0.0, got[0:1, :], got[1:2, :])
    writes[3].start()
    for write in writes:
        write.wait()


def shards(out_grad, routes, gates, pre_gate, pre_up, down_weight):
    dp, wide, narrow = (lax.axis_size(a) for a in ("dp", "wide", "narrow"))
    tok, feat = out_grad.shape
    top = routes.shape[1]
    slots, hid = pre_gate.shape[2:]
    dims = (dp, wide, narrow, tok, top, feat, hid, slots)
    vmem, dma = pltpu.VMEM, pltpu.SemaphoreType.DMA
    any_spec = pl.BlockSpec(memory_space=pl.ANY)
    inputs = (out_grad, routes.T, gates.T, pre_gate[0, 0], pre_up[0, 0], down_weight[0])
    made = pl.pallas_call(
        functools.partial(kernel, dims),
        out_shape=(
            vmem((hid, feat // dp), BF16),
            vmem((slots, hid), BF16),
            vmem((slots, hid), BF16),
            vmem((narrow, 2, LANES), F32),
            vmem((top, LANES), F32),
        ),
        in_specs=[any_spec] * 6,
        out_specs=(any_spec,) * 5,
        scratch_shapes=[
            vmem((top, tok), jnp.int32),
            vmem((top, tok), BF16),
            vmem((slots, hid), BF16),
            vmem((slots, hid), BF16),
            vmem((hid, feat), BF16),
            vmem((dp, 2 * tok, LANES), BF16),
            vmem((tok, LANES), BF16),
            vmem((top, LANES), jnp.int32),
            vmem((top, LANES), F32),
            vmem((LANES, LANES), F32),
            vmem((top, LANES), F32),
            vmem((slots, hid), BF16),
            vmem((slots, hid), F32),
            vmem((slots, hid), F32),
            vmem((dp, narrow, 2 * tok, LANES), BF16),
            vmem((narrow, tok, LANES), BF16),
            vmem((slots, narrow * tok), BF16),
            vmem((dp, wide, 2 * tok, LANES), BF16),
            vmem((dp, wide, 2 * tok, LANES), BF16),
            vmem((wide, 1, LANES), F32),
            vmem((wide, 1, LANES), F32),
            vmem((slots, LANES), F32),
            vmem((hid, slots), BF16),
            vmem((slots, hid), F32),
            vmem((dp - 1, 2, hid, LANES), BF16),
            vmem((dp - 1, 2, hid, LANES), BF16),
            vmem((2, hid, LANES), F32),
            vmem((hid, 2 * LANES), BF16),
            vmem((wide, 1, LANES), F32),
            vmem((wide, 1, LANES), F32),
            vmem((narrow, 2, LANES), F32),
            vmem((narrow, 2, LANES), F32),
            dma((2,)),
            dma((3,)),
            dma,
            dma,
            dma((dp,)),
            dma,
            dma,
            dma,
            dma((dp,)),
            dma,
            dma,
            dma,
            dma((dp - 1, 2, SUBS)),
            dma,
            dma,
            dma,
            dma,
            dma((4,)),
            dma((SUBS,)),
        ],
        compiler_params=pltpu.CompilerParams(collective_id=0, has_side_effects=True),
        name="routed_backward",
    )(*inputs)
    big = made[:3]
    down, dgate, dup, droute = pl.pallas_call(
        functools.partial(hand_on, wide, narrow),
        out_shape=tuple(jax.ShapeDtypeStruct(a.shape, a.dtype) for a in big)
        + (jax.ShapeDtypeStruct((top, tok), F32),),
        in_specs=[any_spec] * 6,
        out_specs=(any_spec,) * 4,
        scratch_shapes=[
            vmem((narrow, 2, LANES), F32),
            vmem((top, LANES), F32),
            vmem((top, tok), jnp.int32),
            vmem((top, tok), F32),
            dma((3,)),
            dma((4,)),
        ],
        compiler_params=pltpu.CompilerParams(vmem_limit_bytes=8 << 20),
        name="hand_on",
    )(*made, routes.T)
    return down[None], dgate[None, None], dup[None, None], droute.T


def solution(mesh):
    placed = (
        P(("dp", "wide", "narrow"), None),
        P(("dp", "wide", "narrow"), None),
        P(("dp", "wide", "narrow"), None),
        P("dp", ("wide", "narrow"), None, None),
        P("dp", ("wide", "narrow"), None, None),
        P(("wide", "narrow"), None, None),
    )
    return jax.shard_map(
        shards,
        mesh=mesh,
        in_specs=placed,
        out_specs=(
            P(("wide", "narrow"), None, "dp"),
            P("dp", ("wide", "narrow"), None, None),
            P("dp", ("wide", "narrow"), None, None),
            P(("dp", "wide", "narrow"), None),
        ),
        check_vma=False,
    )
```

```python
import functools

import jax
import jax.numpy as jnp
from jax import lax
from jax.experimental import pallas as pl
from jax.experimental.pallas import tpu as pltpu
from jax.sharding import PartitionSpec as P

MESH = pl.DeviceIdType.MESH
F32 = jnp.float32
BF16 = jnp.bfloat16
LANES = 128
SUBS = 4
FINISH = 1
NT = (((1,), (1,)), ((), ()))


def iota(shape, dim):
    return lax.broadcasted_iota(jnp.int32, shape, dim)


def kernel(
    dims,
    grads_hbm, routes_hbm, gates_hbm, gate_hbm, up_hbm, weight_hbm,
    down_out, dgate_out, dup_out, pack_res, place_out,
    routes_v, gates_v, gate_v, up_v, weight_v, tokens, table, routes_pad, gates_pad, ranks, place,
    hidden, factor_a, factor_b, gathered, tables, choose,
    rows_out, rows_in, gate_send, gate_recv, gate_rows, scaled_t, back_prop,
    part_out, part_in, part_sum, down_v, slot_out, slot_in, pack_out, pack_in,
    small_sem, load_sem, token_sem, token_send, token_recv, table_send, table_recv,
    rows_send, rows_recv, gates_send, gates_recv, part_send, part_recv,
    slot_send, slot_recv, pack_send, pack_recv, store_sem, down_sem,
):
    dp, wide, narrow, tok, top, feat, hid, slots = dims
    me_x, me_w, me_n = (lax.axis_index(a) for a in ("dp", "wide", "narrow"))
    right, left = lax.rem(me_x + 1, dp), lax.rem(me_x + dp - 1, dp)
    sub_rows = hid // SUBS
    blocks = hid // LANES

    def columns(step):
        first = lax.rem(me_x + (2 * dp - 1) - step, dp) * (2 * LANES)
        second = lax.rem(me_x + 1 + step, dp) * (2 * LANES) + LANES
        return pl.multiple_of(first, LANES), pl.multiple_of(second, LANES)

    def whole(ref, sem):
        pltpu.make_async_copy(ref, ref, sem).wait()

    small = [
        pltpu.make_async_copy(src, dst, small_sem.at[k])
        for k, (src, dst) in enumerate(((routes_hbm, routes_v), (gates_hbm, gates_v)))
    ]
    for load in small:
        load.start()

    near = sorted(range(1, narrow), key=lambda k: -min(k, narrow - k))
    far = sorted(range(1, wide), key=lambda k: -min(k, wide - k))
    barrier = pltpu.get_barrier_semaphore()
    for k in near:
        pl.semaphore_signal(
            barrier, inc=1, device_id={"narrow": lax.rem(me_n + k, narrow)}, device_id_type=MESH
        )
    for k in far:
        pl.semaphore_signal(
            barrier, inc=1, device_id={"wide": lax.rem(me_w + k, wide)}, device_id_type=MESH
        )
    for peer in (right, left):
        pl.semaphore_signal(barrier, inc=1, device_id={"dp": peer}, device_id_type=MESH)

    for step in range(dp):
        for half, col in enumerate(columns(step)):
            pltpu.make_async_copy(
                grads_hbm.at[:, pl.ds(col, LANES)],
                tokens.at[step, pl.ds(half * tok, tok)],
                token_sem,
            ).start()
    loads = [
        pltpu.make_async_copy(src, dst, load_sem.at[k])
        for k, (src, dst) in enumerate(
            ((gate_hbm, gate_v), (up_hbm, up_v), (weight_hbm, weight_v))
        )
    ]

    routes_pad[...] = jnp.full((top, LANES), -1, jnp.int32)
    gates_pad[...] = jnp.zeros((top, LANES), F32)
    for load in small:
        load.wait()
    routes_pad[:, 0:tok] = routes_v[...]
    gates_pad[:, 0:tok] = gates_v[...].astype(F32)
    square = (LANES, LANES)
    expert_row = iota(square, 0)
    hits = jnp.zeros(square, F32)
    gate_at = jnp.zeros(square, F32)
    for k in range(top):
        same = routes_pad[k : k + 1, :] == expert_row
        hits = jnp.where(same, 1.0, hits)
        gate_at = jnp.where(same, gates_pad[k : k + 1, :], gate_at)
    earlier = jnp.where(iota(square, 0) < iota(square, 1), 1.0, 0.0).astype(BF16)
    before = jnp.dot(hits.astype(BF16), earlier, preferred_element_type=F32)
    ranks[...] = before
    unit = jnp.where(iota((tok, LANES), 0) == iota((tok, LANES), 1), 1.0, 0.0).astype(BF16)
    held = jnp.where(before == 0.0, gate_at, jnp.where(before == 1.0, -gate_at, 0.0)).astype(BF16)
    table[...] = lax.dot_general(unit, held, NT, preferred_element_type=F32).astype(BF16)

    pl.semaphore_wait(barrier, (narrow - 1) + (wide - 1) + 2)

    def to_narrow(src, dst, send, recv):
        for k in near:
            pltpu.make_async_remote_copy(
                src_ref=src, dst_ref=dst.at[me_n], send_sem=send, recv_sem=recv,
                device_id={"narrow": lax.rem(me_n + k, narrow)}, device_id_type=MESH,
            ).start()
        pltpu.make_async_copy(src, dst.at[me_n], recv).start()

    def to_wide(src, dst, send, recv):
        for k in far:
            peer = lax.rem(me_w + k, wide)
            pltpu.make_async_remote_copy(
                src_ref=src.at[peer], dst_ref=dst.at[me_w], send_sem=send, recv_sem=recv,
                device_id={"wide": peer}, device_id_type=MESH,
            ).start()
        pltpu.make_async_copy(src.at[me_w], dst.at[me_w], recv).start()

    def spread(step):
        to_narrow(tokens.at[step], gathered.at[step], token_send, token_recv.at[step])

    to_narrow(table, tables, table_send, table_recv)
    whole(tokens, token_sem)
    for step in range(4):
        spread(step)
    for load in loads:
        load.start()

    whole(tables, table_recv)
    shape = (slots, narrow * tok)
    slot_row, entry = iota(shape, 0), iota(shape, 1)
    pick = jnp.where(entry == (slot_row >> 4) * narrow + me_n, 1.0, 0.0).astype(BF16)
    full = lax.dot_general(
        pick, tables[...].reshape(narrow * tok, LANES), NT, preferred_element_type=F32
    )
    mine = ((slot_row >> 1) & (narrow - 1)) == (entry >> 4)
    signed = jnp.where((slot_row & 1) == 0, full, -full)
    gate_of = jnp.where(mine, jnp.maximum(signed, 0.0), 0.0)
    choose[...] = jnp.where(gate_of > 0.0, 1.0, 0.0).astype(BF16)

    cube = (wide, 2 * narrow, LANES)
    diagonal = iota(cube, 1) == iota(cube, 2)

    def to_lanes(column):
        spread_out = jnp.broadcast_to(column, (slots, LANES)).reshape(cube)
        return jnp.sum(jnp.where(diagonal, spread_out, 0.0), axis=1, keepdims=True)

    def to_rows(lanes):
        spread_out = jnp.where(diagonal, jnp.broadcast_to(lanes, cube), 0.0)
        return jnp.broadcast_to(jnp.sum(spread_out, axis=2, keepdims=True), cube)

    gate_send[...] = to_lanes(jnp.sum(gate_of, axis=1, keepdims=True))
    to_wide(gate_send, gate_recv, gates_send, gates_recv)

    def forward(step):
        whole(gathered.at[step], token_recv.at[step])
        for half in range(2):
            held = gathered[step, :, half * tok : (half + 1) * tok, :].reshape(narrow * tok, LANES)
            picked = jnp.dot(choose[...], held, preferred_element_type=F32).astype(BF16)
            rows_out[step, :, half * tok : (half + 1) * tok, :] = picked.reshape(
                wide, 2 * narrow, LANES
            )
        to_wide(rows_out.at[step], rows_in.at[step], rows_send, rows_recv.at[step])

    forward(0)
    spread(4)
    spread(5)

    for k in range(top):
        same = routes_pad[k : k + 1, :] == expert_row
        place[k : k + 1, :] = jnp.sum(jnp.where(same, ranks[...], 0.0), axis=0, keepdims=True)
    for load in loads[:2]:
        load.wait()

    @pl.loop(0, blocks)
    def _(b):
        col = pl.ds(pl.multiple_of(b * LANES, LANES), LANES)
        gate = gate_v[:, col].astype(F32)
        up = up_v[:, col].astype(F32)
        sig = jax.nn.sigmoid(gate)
        silu = gate * sig
        hidden[:, col] = (silu * up).astype(BF16)
        factor_a[:, col] = up * sig * (1.0 + gate * (1.0 - sig))
        factor_b[:, col] = silu

    forward(1)
    spread(6)
    spread(7)

    whole(gate_recv, gates_recv)
    gate_rows[...] = to_rows(gate_recv[...]).reshape(slots, LANES)
    for b in range(blocks):
        col = slice(b * LANES, (b + 1) * LANES)
        scaled = (gate_rows[...] * hidden[:, col].astype(F32)).astype(BF16).astype(F32)
        scaled_t[b * LANES : (b + 1) * LANES, :] = scaled.T.astype(BF16)
    back_prop[...] = jnp.zeros_like(back_prop)

    def rows(step, half):
        return rows_in[step, :, half * tok : (half + 1) * tok, :].reshape(slots, LANES)

    def arrive(step):
        whole(rows_in.at[step], rows_recv.at[step])

    def partial_of(step):
        for half in range(2):
            part_sum[half] = jnp.dot(scaled_t[...], rows(step, half), preferred_element_type=F32)

    def copy_of(step, half, sub, peer):
        at = pl.ds(sub * sub_rows, sub_rows)
        return pltpu.make_async_remote_copy(
            src_ref=part_out.at[step, half, at],
            dst_ref=part_in.at[step, half, at],
            send_sem=part_send,
            recv_sem=part_recv.at[step, half, sub],
            device_id={"dp": peer},
            device_id_type=MESH,
        )

    def ring(step, first, between=None, when=0):
        partial_of(step)
        for sub in range(SUBS):
            if sub == when and between is not None:
                between()
            at = slice(sub * sub_rows, (sub + 1) * sub_rows)
            for half, peer in enumerate((right, left)):
                value = part_sum[half, at, :]
                if not first:
                    copy_of(step - 1, half, sub, peer).wait_recv()
                    value = value + part_in[step - 1, half, at, :].astype(F32)
                part_out[step, half, at, :] = value.astype(BF16)
                copy_of(step, half, sub, peer).start()

    def back(step):
        total = back_prop[...]
        for half, col in enumerate(columns(step)):
            total = total + lax.dot_general(
                rows(step, half), weight_v[:, pl.ds(col, LANES)], NT, preferred_element_type=F32
            )
        back_prop[...] = total

    arrive(0)
    ring(0, True)
    pl.loop(2, 5)(forward)
    loads[2].wait()
    back(0)

    @pl.loop(1, 3)
    def _(step):
        arrive(step)
        ring(step, False)
        pl.loop(2 * step + 3, jnp.minimum(2 * step + 5, dp))(forward)
        back(step)

    @pl.loop(3, dp - 3)
    def _(step):
        arrive(step)
        ring(step, False)
        back(step)

    stores = [
        pltpu.make_async_copy(gate_v, dgate_out, store_sem.at[0]),
        pltpu.make_async_copy(up_v, dup_out, store_sem.at[1]),
    ]

    def finish():
        back(dp - 3)
        for step in (dp - 2, dp - 1):
            arrive(step)
            back(step)
        dots = jnp.zeros((slots, LANES), F32)
        for b in range(blocks):
            col = slice(b * LANES, (b + 1) * LANES)
            dots = dots + hidden[:, col].astype(F32) * back_prop[:, col]
        slot_out[...] = to_lanes(jnp.sum(dots, axis=1, keepdims=True))
        to_wide(slot_out, slot_in, slot_send, slot_recv)

    arrive(dp - 3)
    ring(dp - 3, False, finish, FINISH)
    for b in range(blocks):
        col = slice(b * LANES, (b + 1) * LANES)
        carried = gate_rows[...] * back_prop[:, col]
        gate_v[:, col] = (carried * factor_a[:, col]).astype(BF16)
        up_v[:, col] = (carried * factor_b[:, col]).astype(BF16)
    for store in stores:
        store.start()
    placed_out = pltpu.make_async_copy(place, place_out, store_sem.at[2])
    placed_out.start()
    ring(dp - 2, False)

    whole(slot_in, slot_recv)
    here = iota(cube, 2) == me_n * wide + iota(cube, 0)
    packed = jnp.sum(jnp.where(here, to_rows(slot_in[...]), 0.0), axis=0)
    for k in range(2 * narrow):
        pack_out[k // 2, k % 2 : k % 2 + 1, :] = packed[k : k + 1, :]
    for k in near:
        peer = lax.rem(me_n + k, narrow)
        pltpu.make_async_remote_copy(
            src_ref=pack_out.at[peer], dst_ref=pack_in.at[me_n],
            send_sem=pack_send, recv_sem=pack_recv,
            device_id={"narrow": peer}, device_id_type=MESH,
        ).start()
    pltpu.make_async_copy(pack_out.at[me_n], pack_in.at[me_n], pack_recv).start()

    downs = []
    partial_of(dp - 1)
    for sub in range(SUBS):
        at = slice(sub * sub_rows, (sub + 1) * sub_rows)
        for half, peer in enumerate((right, left)):
            copy_of(dp - 2, half, sub, peer).wait_recv()
            value = part_sum[half, at, :] + part_in[dp - 2, half, at, :].astype(F32)
            down_v[at, half * LANES : (half + 1) * LANES] = value.astype(BF16)
        sends = pltpu.make_async_copy(
            down_v.at[pl.ds(sub * sub_rows, sub_rows)],
            down_out.at[pl.ds(sub * sub_rows, sub_rows)],
            down_sem.at[sub],
        )
        sends.start()
        downs.append(sends)

    whole(pack_in, pack_recv)
    packs = pltpu.make_async_copy(pack_in, pack_res, store_sem.at[3])
    packs.start()

    for store in stores:
        store.wait()
    placed_out.wait()
    packs.wait()
    for send in downs:
        send.wait()
    peers_n, peers_w = pl.ds(0, narrow - 1), pl.ds(0, wide - 1)
    for step in range(dp):
        whole(gathered.at[step, peers_n], token_send)
        whole(rows_in.at[step, peers_w], rows_send)
    whole(tables.at[peers_n], table_send)
    whole(gate_recv.at[peers_w], gates_send)
    whole(slot_in.at[peers_w], slot_send)
    whole(pack_in.at[peers_n], pack_send)
    whole(part_in, part_send)


def hand_on(wide, narrow, *refs):
    sources, small, targets, route_out = refs[0:3], refs[3:6], refs[6:9], refs[9]
    held, result, taken, given = refs[10:13], refs[13], refs[14], refs[15]
    pack, place, routes = held
    writes = [
        pltpu.make_async_copy(a, b, given.at[k])
        for k, (a, b) in enumerate([*zip(sources, targets), (result, route_out)])
    ]
    reads = [pltpu.make_async_copy(a, b, taken.at[k]) for k, (a, b) in enumerate(zip(small, held))]
    for copy in reads + writes[:3]:
        copy.start()
    for read in reads:
        read.wait()
    top, tok = result.shape
    rows = jnp.sum(pack[...], axis=0)
    for k in range(top):
        named = routes[k : k + 1, :]
        lane = (named & (narrow - 1)) * wide + (named >> 3)
        one = jnp.where(lane == iota((LANES, tok), 0), 1.0, 0.0)
        got = jnp.dot(rows, one, precision=lax.Precision.HIGHEST, preferred_element_type=F32)
        result[k : k + 1, :] = jnp.where(place[k : k + 1, 0:tok] == 0.0, got[0:1, :], got[1:2, :])
    writes[3].start()
    for write in writes:
        write.wait()


def shards(out_grad, routes, gates, pre_gate, pre_up, down_weight):
    dp, wide, narrow = (lax.axis_size(a) for a in ("dp", "wide", "narrow"))
    tok, feat = out_grad.shape
    top = routes.shape[1]
    slots, hid = pre_gate.shape[2:]
    dims = (dp, wide, narrow, tok, top, feat, hid, slots)
    vmem, dma = pltpu.VMEM, pltpu.SemaphoreType.DMA
    any_spec = pl.BlockSpec(memory_space=pl.ANY)
    inputs = (out_grad, routes.T, gates.T, pre_gate[0, 0], pre_up[0, 0], down_weight[0])
    made = pl.pallas_call(
        functools.partial(kernel, dims),
        out_shape=(
            vmem((hid, feat // dp), BF16),
            vmem((slots, hid), BF16),
            vmem((slots, hid), BF16),
            vmem((narrow, 2, LANES), F32),
            vmem((top, LANES), F32),
        ),
        in_specs=[any_spec] * 6,
        out_specs=(any_spec,) * 5,
        scratch_shapes=[
            vmem((top, tok), jnp.int32),
            vmem((top, tok), BF16),
            vmem((slots, hid), BF16),
            vmem((slots, hid), BF16),
            vmem((hid, feat), BF16),
            vmem((dp, 2 * tok, LANES), BF16),
            vmem((tok, LANES), BF16),
            vmem((top, LANES), jnp.int32),
            vmem((top, LANES), F32),
            vmem((LANES, LANES), F32),
            vmem((top, LANES), F32),
            vmem((slots, hid), BF16),
            vmem((slots, hid), F32),
            vmem((slots, hid), F32),
            vmem((dp, narrow, 2 * tok, LANES), BF16),
            vmem((narrow, tok, LANES), BF16),
            vmem((slots, narrow * tok), BF16),
            vmem((dp, wide, 2 * tok, LANES), BF16),
            vmem((dp, wide, 2 * tok, LANES), BF16),
            vmem((wide, 1, LANES), F32),
            vmem((wide, 1, LANES), F32),
            vmem((slots, LANES), F32),
            vmem((hid, slots), BF16),
            vmem((slots, hid), F32),
            vmem((dp - 1, 2, hid, LANES), BF16),
            vmem((dp - 1, 2, hid, LANES), BF16),
            vmem((2, hid, LANES), F32),
            vmem((hid, 2 * LANES), BF16),
            vmem((wide, 1, LANES), F32),
            vmem((wide, 1, LANES), F32),
            vmem((narrow, 2, LANES), F32),
            vmem((narrow, 2, LANES), F32),
            dma((2,)),
            dma((3,)),
            dma,
            dma,
            dma((dp,)),
            dma,
            dma,
            dma,
            dma((dp,)),
            dma,
            dma,
            dma,
            dma((dp - 1, 2, SUBS)),
            dma,
            dma,
            dma,
            dma,
            dma((4,)),
            dma((SUBS,)),
        ],
        compiler_params=pltpu.CompilerParams(collective_id=0, has_side_effects=True),
        name="routed_backward",
    )(*inputs)
    big = made[:3]
    down, dgate, dup, droute = pl.pallas_call(
        functools.partial(hand_on, wide, narrow),
        out_shape=tuple(jax.ShapeDtypeStruct(a.shape, a.dtype) for a in big)
        + (jax.ShapeDtypeStruct((top, tok), F32),),
        in_specs=[any_spec] * 6,
        out_specs=(any_spec,) * 4,
        scratch_shapes=[
            vmem((narrow, 2, LANES), F32),
            vmem((top, LANES), F32),
            vmem((top, tok), jnp.int32),
            vmem((top, tok), F32),
            dma((3,)),
            dma((4,)),
        ],
        compiler_params=pltpu.CompilerParams(vmem_limit_bytes=8 << 20),
        name="hand_on",
    )(*made, routes.T)
    return down[None], dgate[None, None], dup[None, None], droute.T


def solution(mesh):
    placed = (
        P(("dp", "wide", "narrow"), None),
        P(("dp", "wide", "narrow"), None),
        P(("dp", "wide", "narrow"), None),
        P("dp", ("wide", "narrow"), None, None),
        P("dp", ("wide", "narrow"), None, None),
        P(("wide", "narrow"), None, None),
    )
    return jax.shard_map(
        shards,
        mesh=mesh,
        in_specs=placed,
        out_specs=(
            P(("wide", "narrow"), None, "dp"),
            P("dp", ("wide", "narrow"), None, None),
            P("dp", ("wide", "narrow"), None, None),
            P(("dp", "wide", "narrow"), None),
        ),
        check_vma=False,
    )
```
